128 devices in a mesh: bank: 4 (over y_hi, core), gal: 32 (over z, y_lo, x).
Axes of the slice: x: 4, y: 4 (y_hi: 2, y_lo: 2; y = y_hi * 2 + y_lo), z: 4, core: 2. Of those that a mesh axis runs over, the one named last changes fastest.
Arguments:
- querybank: bfloat16 [16384, 512], P(('bank', 'gal')), may hold values from -80 to 80
- gallery: bfloat16 [131072, 512], P('gal'), may hold values from -80 to 80
- test_queries: bfloat16 [2048, 512], P(('bank', 'gal')), may hold values from -80 to 80
Outputs:
- retrieval: float32 [2048, 32, 4096], P(None, 'gal', 'bank')
The draws below stay inside these ranges and needn't reach their ends.
All inputs are finite; a program needn't handle non-finite values.
Results may differ from the reference program's by a relative error of at most 0.0017.
Values may be sent and summed in bfloat16 or wider, within the bound.
A program may use at most 64 MiB of HBM per device.

```python
import math
import jax
import jax.numpy as jnp
from jax import lax

D = 512
CLIP_GAL = 4096
CLIPS = 131072
BANK = 16384
TESTQ = 2048
N_BANK = 4
N_GAL = 32


def embed_rows(key, row_count, tag):
    topics = max(BANK // 64, 4)
    shared = jax.random.fold_in(key, 5)
    centre_key, column_key = jax.random.split(shared)
    row_key = jax.random.fold_in(key, tag)
    pick_key, noise_key, mixing_key, scale_key = jax.random.split(row_key, 4)
    topic_ids = jax.random.randint(pick_key, (row_count,), 0, topics)
    centroids = jax.random.truncated_normal(centre_key, -3.0, 3.0, (topics, D), jnp.float32)
    col_scale = jnp.exp(jax.random.uniform(column_key, (1, D), jnp.float32, math.log(0.5), math.log(2.0)))
    noise_part = jax.random.truncated_normal(noise_key, -3.0, 3.0, (row_count, D), jnp.float32)
    mixing = jax.random.uniform(mixing_key, (row_count, 1), jnp.float32, 0.5, 1.1)
    row_scale = jnp.exp(jax.random.uniform(scale_key, (row_count, 1), jnp.float32, 0.0, math.log(6.0)))
    base_rows = mixing * jnp.take(centroids, topic_ids, axis=0) + noise_part
    return (base_rows * row_scale * col_scale).astype(jnp.bfloat16)


def draw_querybank(key, part):
    return embed_rows(key, BANK, 11)


def draw_gallery(key, part):
    return embed_rows(key, CLIPS, 23)


def draw_test_queries(key, part):
    return embed_rows(key, TESTQ, 37)


def setup_inputs(seed: int = 0) -> dict:
    key_list = jax.random.split(jax.random.key(seed), 4)
    querybank = draw_querybank(jax.random.fold_in(key_list[3], 71), 0)
    gallery = draw_gallery(jax.random.fold_in(key_list[3], 71), 0)
    test_queries = draw_test_queries(jax.random.fold_in(key_list[3], 71), 0)
    return dict(querybank=querybank, gallery=gallery, test_queries=test_queries)


inverse_temp = 20.0
epsilon = 1e-06

def unit_rows(values):
    wide = values.astype(jnp.float32)
    return (wide * lax.rsqrt(lax.optimization_barrier(jnp.sum(wide * wide, axis=-1, keepdims=True)) + epsilon)).astype(jnp.bfloat16)

def reference(querybank, gallery, test_queries):
    captions = unit_rows(querybank).reshape(N_BANK, BANK // N_BANK, D)
    clips = unit_rows(gallery).reshape(N_GAL, CLIP_GAL, D)
    tests = unit_rows(test_queries)

    def per_shard(block):
        block_t = block.T

        def per_group(group):
            sims = jnp.dot(group, block_t, preferred_element_type=jnp.float32)
            return lax.optimization_barrier(jnp.sum(jnp.exp(inverse_temp * sims), axis=0))
        normalizer = lax.optimization_barrier(jnp.sum(lax.map(per_group, captions), axis=0))
        scores = jnp.dot(tests, block_t, preferred_element_type=jnp.float32)
        return inverse_temp * scores - jnp.log(normalizer / BANK)[None, :]
    shards = lax.map(per_shard, clips)
    return jnp.transpose(shards, (1, 0, 2))
```

```python
import functools
import math

import jax
import jax.numpy as jnp
from jax import lax
from jax.experimental import pallas as pl
from jax.experimental.pallas import tpu as pltpu
from jax.sharding import PartitionSpec as P

MESH = pl.DeviceIdType.MESH
inverse_temp = 20.0
epsilon = 1e-06
exp2_scale = inverse_temp * math.log2(math.e)

D = 512
PIECE = 64
GROUP = 4
RING = 4


def piece_table():
    ring_hops = (0, 1, 2, 1)
    pieces = [
        (kind, dy, p1, p2)
        for dy in range(2)
        for p1 in range(RING)
        for p2 in range(RING)
        for kind in range(2)
    ]

    def depth(piece):
        return piece[1] + ring_hops[piece[2]] + ring_hops[piece[3]]

    def way(piece):
        kind, dy, p1, p2 = piece
        if p2:
            side = p2 if p2 != 2 else (1 if (dy + p1) % 2 == 0 else 3)
            parent = (kind, dy, p1, (p2 - side) % RING)
            return parent, ("x", "z")[1 - kind], side
        if p1:
            side = p1 if p1 != 2 else (1 if dy == 0 else 3)
            parent = (kind, dy, (p1 - side) % RING, 0)
            return parent, ("x", "z")[kind], side
        if dy:
            return (kind, 0, 0, 0), "y", 1
        return None

    pieces.sort(key=lambda q: (depth(q), q[3] != 0, q[2] != 0, q[1], q[2], q[3], q[0]))
    slot = {q: s for s, q in enumerate(pieces)}
    children = [[] for _ in pieces]
    for q in pieces:
        came = way(q)
        if came is not None:
            parent, axis, side = came
            children[slot[parent]].append((slot[q], axis, -side))
    return children


CHILDREN = piece_table()
PIECES = len(CHILDREN)
STEPS = PIECES // GROUP


def unit_scale(wide):
    return lax.rsqrt(jnp.sum(wide * wide, axis=-1, keepdims=True) + epsilon)


def unit_kernel(caps_ref, tests_ref, caps_out, tests_out):
    wide = caps_ref[...].astype(jnp.float32)
    caps_out[...] = (wide * (unit_scale(wide) * exp2_scale)).astype(jnp.bfloat16)
    wide = tests_ref[...].astype(jnp.float32)
    tests_out[...] = (wide * unit_scale(wide)).astype(jnp.bfloat16)


def gather_kernel(
    caps_ref, tests_ref, gallery_ref, all_tests_ref, columns_ref, log_ref,
    caps, tests, clips, acc, share, others,
    send_sem, recv_sem, tsend_sem, trecv_sem, bsend_sem, brecv_sem, local_sem,
):
    bank = lax.axis_index("bank")
    gal = lax.axis_index("gal")
    y_hi, core = bank // 2, bank % 2
    z, y_lo, x = gal // 8, (gal // 4) % 2, gal % 4
    y = y_hi * 2 + y_lo

    def at(axis, step):
        if axis == "x":
            return {"bank": bank, "gal": z * 8 + y_lo * 4 + (x + step + 4) % 4}
        if axis == "z":
            return {"bank": bank, "gal": ((z + step + 4) % 4) * 8 + y_lo * 4 + x}
        new_y = (y + step + 4) % 4
        return {"bank": (new_y // 2) * 2 + core, "gal": z * 8 + (new_y % 2) * 4 + x}

    partner = {"bank": bank, "gal": z * 8 + (1 - y_lo) * 4 + x}
    sibling = {"bank": y_hi * 2 + 1 - core, "gal": gal}

    load = pltpu.make_async_copy(gallery_ref, clips, local_sem.at[0])
    load.start()

    barrier = pltpu.get_barrier_semaphore()
    peers = [at("x", 1), at("x", -1), at("z", 1), at("z", -1), at("y", 1), at("y", -1)]
    peers += [{"bank": (bank + k) % 4, "gal": gal} for k in (1, 2, 3)]
    for peer in peers:
        pl.semaphore_signal(barrier, inc=1, device_id=peer, device_id_type=MESH)
    pl.semaphore_wait(barrier, len(peers))

    def send_of(source, target, axis, step):
        device = partner if axis == "y" else at(axis, step)
        return pltpu.make_async_remote_copy(
            src_ref=source,
            dst_ref=caps.at[target],
            send_sem=send_sem.at[target],
            recv_sem=recv_sem.at[target],
            device_id=device,
            device_id_type=MESH,
        )

    def own(piece):
        return caps_ref.at[pl.ds(piece * PIECE, PIECE), :]

    def forward(piece):
        source = own(piece) if piece < 2 else caps.at[piece]
        for target, axis, step in CHILDREN[piece]:
            send_of(source, target, axis, step).start()

    def arrive(piece):
        send_of(caps.at[piece], piece, "x", 1).wait_recv()
        forward(piece)

    def test_copy(index, part, device):
        return pltpu.make_async_remote_copy(
            src_ref=part, dst_ref=part,
            send_sem=tsend_sem.at[index], recv_sem=trecv_sem.at[index],
            device_id=device, device_id_type=MESH,
        )

    def minus(value, step):
        return (value - step + 4) % 4

    def y_block(value):
        return tests.at[(value // 2) * 2 + core, :, value % 2]

    def y_half(value, half):
        return tests.at[(value // 2) * 2 + core, pl.ds(half * 2, 2), value % 2]

    def test_sends(stage):
        mine = tests.at[bank, z, y_lo, x]
        if stage == 0:
            return [(0, tests_ref, mine, at("x", 1)), (1, tests_ref, mine, at("x", -1))]
        if stage == 1:
            part = tests.at[bank, z, y_lo, minus(x, 1)]
            return [(2, part, part, at("x", 1))]
        if stage == 2:
            part = tests.at[bank, z, y_lo]
            return [(3, part, part, at("z", 1)), (4, part, part, at("z", -1))]
        if stage == 3:
            up = tests.at[bank, minus(z, 1), y_lo, pl.ds(0, 2)]
            down = tests.at[bank, minus(z, -1), y_lo, pl.ds(2, 2)]
            return [(5, up, up, at("z", 1)), (6, down, down, at("z", -1))]
        if stage == 4:
            part = y_block(y)
            return [(7, part, part, at("y", 1)), (8, part, part, at("y", -1))]
        if stage == 5:
            up, down = y_half(minus(y, 1), 0), y_half(minus(y, -1), 1)
            return [(9, up, up, at("y", 1)), (10, down, down, at("y", -1))]
        low, high = tests.at[core], tests.at[2 + core]
        return [(11, low, low, sibling), (12, high, high, sibling)]

    def test_start(stage):
        for index, source, target, device in test_sends(stage):
            pltpu.make_async_remote_copy(
                src_ref=source, dst_ref=target,
                send_sem=tsend_sem.at[index], recv_sem=trecv_sem.at[index],
                device_id=device, device_id_type=MESH,
            ).start()

    def test_arrive(stage):
        for index, source, target, device in test_sends(stage):
            if stage == 0:
                part = tests.at[bank, z, y_lo, minus(x, 1 if index == 0 else -1)]
            elif stage == 1:
                part = tests.at[bank, z, y_lo, minus(x, 2)]
            elif stage == 2:
                part = tests.at[bank, minus(z, 1 if index == 3 else -1), y_lo]
            elif stage == 3:
                part = tests.at[bank, minus(z, 2), y_lo, pl.ds(0 if index == 5 else 2, 2)]
            elif stage == 4:
                part = y_block(minus(y, 1 if index == 7 else -1))
            elif stage == 5:
                part = y_half(minus(y, 2), 0 if index == 9 else 1)
            else:
                part = tests.at[(0 if index == 11 else 2) + 1 - core]
            test_copy(index, part, sibling).wait_recv()

    forward(0)
    forward(1)
    test_start(0)
    caps[0] = caps_ref[0:PIECE, :]
    caps[1] = caps_ref[PIECE : 2 * PIECE, :]
    tests[bank, z, y_lo, x] = tests_ref[...]
    acc[...] = jnp.zeros_like(acc)

    load.wait()

    def unit_block(index, carry):
        rows = pl.ds(pl.multiple_of(index * 256, 256), 256)
        wide = clips[rows, :].astype(jnp.float32)
        clips[rows, :] = (wide * unit_scale(wide)).astype(jnp.bfloat16)
        return carry

    lax.fori_loop(0, clips.shape[0] // 256, unit_block, 0)

    share_rows = columns_ref.shape[0]
    columns_copy = pltpu.make_async_copy(
        clips.at[pl.ds(pl.multiple_of(bank * share_rows, share_rows), share_rows), :],
        columns_ref,
        local_sem.at[1],
    )

    test_steps = {2: 0, 3: 1, 5: 2, 7: 3, 11: 4, 14: 5}

    def move(step):
        for piece in range(GROUP * step, GROUP * (step + 1)):
            if piece >= 2:
                arrive(piece)
        if step == 1:
            columns_copy.start()
        if step in test_steps:
            test_arrive(test_steps[step])
            test_start(test_steps[step] + 1)

    def choose(step, low, high):
        if high - low == 1:
            move(low)
            return
        middle = (low + high) // 2

        @pl.when(step < middle)
        def _():
            choose(step, low, middle)

        @pl.when(step >= middle)
        def _():
            choose(step, middle, high)

    def one_step(step, carry):
        choose(step, 0, STEPS)
        block = caps[pl.ds(step * GROUP, GROUP)].reshape(GROUP * PIECE, D)
        sims = lax.dot_general(
            block, clips[...], (((1,), (1,)), ((), ())), preferred_element_type=jnp.float32
        )
        terms = jnp.exp2(sims).reshape(GROUP * PIECE // 8, 8, sims.shape[1])
        acc[...] += jnp.sum(terms, axis=0)
        return carry

    lax.fori_loop(0, STEPS, one_step, 0)

    sums = jnp.sum(acc[...], axis=0, keepdims=True)
    for k in range(4):
        share[k] = sums[:, k * share_rows : (k + 1) * share_rows]

    def bank_copy(k):
        peer = (bank + k) % 4
        return pltpu.make_async_remote_copy(
            src_ref=share.at[peer], dst_ref=others.at[k - 1],
            send_sem=bsend_sem.at[k - 1], recv_sem=brecv_sem.at[k - 1],
            device_id={"bank": peer, "gal": gal}, device_id_type=MESH,
        )

    for k in (2, 1, 3):
        bank_copy(k).start()

    test_arrive(6)
    tests_copy = pltpu.make_async_copy(tests, all_tests_ref, local_sem.at[2])
    tests_copy.start()

    for k in (1, 3, 2):
        bank_copy(k).wait_recv()
    total = share[bank] + others[0] + others[1] + others[2]
    count = 4 * 32 * caps_ref.shape[0]
    log_ref[...] = jnp.log(total / count)

    for k in (1, 2, 3):
        bank_copy(k).wait_send()
    for piece in range(PIECES):
        source = own(piece) if piece < 2 else caps.at[piece]
        for target, axis, step in CHILDREN[piece]:
            send_of(source, target, axis, step).wait_send()
    for stage in range(7):
        for index, source, target, device in test_sends(stage):
            test_copy(index, target, device).wait_send()
    columns_copy.wait()
    tests_copy.wait()


def score_kernel(tests_ref, columns_ref, log_ref, out_ref):
    sims = lax.dot_general(
        tests_ref[...], columns_ref[...], (((1,), (1,)), ((), ())), preferred_element_type=jnp.float32
    )
    result = inverse_temp * sims - log_ref[...]
    out_ref[...] = result.reshape(out_ref.shape)


def local(querybank, gallery, test_queries):
    vmem = pl.BlockSpec(memory_space=pltpu.VMEM)
    anywhere = pl.BlockSpec(memory_space=pl.ANY)
    bf16, f32 = jnp.bfloat16, jnp.float32
    clip_rows = gallery.shape[0]
    share_rows = clip_rows // 4
    test_rows = test_queries.shape[0] * 128
    caps, tests = pl.pallas_call(
        unit_kernel,
        out_shape=(
            jax.ShapeDtypeStruct(querybank.shape, bf16),
            jax.ShapeDtypeStruct(test_queries.shape, bf16),
        ),
        in_specs=[vmem, vmem],
        out_specs=(vmem, vmem),
    )(querybank, test_queries)
    tests_shape = (4, 4, 2, 4, test_queries.shape[0], D)
    every_test, columns, logs = pl.pallas_call(
        gather_kernel,
        out_shape=(
            jax.ShapeDtypeStruct(tests_shape, bf16),
            jax.ShapeDtypeStruct((share_rows, D), bf16),
            jax.ShapeDtypeStruct((1, share_rows), f32),
        ),
        in_specs=[vmem, vmem, anywhere],
        out_specs=(anywhere, anywhere, vmem),
        scratch_shapes=[
            pltpu.VMEM((PIECES, PIECE, D), bf16),
            pltpu.VMEM(tests_shape, bf16),
            pltpu.VMEM((clip_rows, D), bf16),
            pltpu.VMEM((8, clip_rows), f32),
            pltpu.VMEM((4, 1, share_rows), f32),
            pltpu.VMEM((3, 1, share_rows), f32),
            pltpu.SemaphoreType.DMA((PIECES,)),
            pltpu.SemaphoreType.DMA((PIECES,)),
            pltpu.SemaphoreType.DMA((13,)),
            pltpu.SemaphoreType.DMA((13,)),
            pltpu.SemaphoreType.DMA((3,)),
            pltpu.SemaphoreType.DMA((3,)),
            pltpu.SemaphoreType.DMA((3,)),
        ],
        compiler_params=pltpu.CompilerParams(
            collective_id=0, has_side_effects=True, vmem_limit_bytes=40 << 20
        ),
    )(caps, tests, gallery)
    block = 256
    result = pl.pallas_call(
        score_kernel,
        grid=(test_rows // block,),
        out_shape=jax.ShapeDtypeStruct((test_rows, 1, share_rows), f32),
        in_specs=[
            pl.BlockSpec((block, D), lambda i: (i, 0)),
            pl.BlockSpec((share_rows, D), lambda i: (0, 0)),
            pl.BlockSpec((1, share_rows), lambda i: (0, 0)),
        ],
        out_specs=pl.BlockSpec((block, 1, share_rows), lambda i: (i, 0, 0)),
        compiler_params=pltpu.CompilerParams(vmem_limit_bytes=40 << 20),
    )(every_test.reshape(test_rows, D), columns, logs)
    return result


def solution(mesh):
    placed = (P(("bank", "gal"), None), P("gal", None), P(("bank", "gal"), None))
    return jax.shard_map(
        local, mesh=mesh, in_specs=placed, out_specs=P(None, "gal", "bank"), check_vma=False
    )
```

```python
import functools
import math

import jax
import jax.numpy as jnp
from jax import lax
from jax.experimental import pallas as pl
from jax.experimental.pallas import tpu as pltpu
from jax.sharding import PartitionSpec as P

MESH = pl.DeviceIdType.MESH
inverse_temp = 20.0
epsilon = 1e-06
exp2_scale = inverse_temp * math.log2(math.e)

D = 512
PIECE = 64
GROUP = 4
RING = 4


ORDER = (
    0, 1, 6, 32, 3, 24, 2, 9, 7, 25, 34, 33, 40, 8, 26, 30,
    11, 15, 57, 56, 17, 38, 5, 39, 14, 48, 41, 62, 35, 13, 27, 16,
    28, 63, 59, 10, 19, 31, 43, 58, 36, 47, 46, 42, 4, 49, 54, 18,
    21, 44, 29, 50, 45, 61, 55, 37, 52, 23, 60, 51, 12, 53, 22, 20,
)
AHEAD = (
    0, 0, 0, 1, 0, 2, 0, 0, 0, 0, 0, 1, 0, 2, 0, 0,
    0, 0, 0, 2, 0, 0, 0, 1, 1, 0, 0, 0, 1, 0, 0, 0,
    0, 0, 0, 0, 1, 2, 0, 2, 0, 0, 1, 2, 2, 2, 0, 0,
    0, 0, 1, 1, 0, 0, 1, 0, 0, 0, 2, 1, 2, 0, 0, 0,
)


def piece_table():
    pieces = [(code % 2, code // 32, code // 8 % 4, code // 2 % 4) for code in ORDER]

    def way(piece):
        kind, dy, p1, p2 = piece
        if p2:
            side = p2 if p2 != 2 else (1 if (dy + p1) % 2 == 0 else 3)
            parent = (kind, dy, p1, (p2 - side) % RING)
            return parent, ("x", "z")[1 - kind], side
        if p1:
            side = p1 if p1 != 2 else (1 if dy == 0 else 3)
            parent = (kind, dy, (p1 - side) % RING, 0)
            return parent, ("x", "z")[kind], side
        if dy:
            return (kind, 0, 0, 0), "y", 1
        return None

    slot = {q: s for s, q in enumerate(pieces)}
    children = [[] for _ in pieces]
    for q in pieces:
        came = way(q)
        if came is not None:
            parent, axis, side = came
            children[slot[parent]].append((slot[q], axis, -side))
    return children


CHILDREN = piece_table()
PIECES = len(CHILDREN)
STEPS = PIECES // GROUP
HANDLED = [
    [s for s in range(2, PIECES) if max(0, s // GROUP - AHEAD[s]) == step] for step in range(STEPS)
]


def unit_scale(wide):
    return lax.rsqrt(jnp.sum(wide * wide, axis=-1, keepdims=True) + epsilon)


def gather_kernel(
    caps_ref, tests_ref, gallery_ref, all_tests_ref, columns_ref, log_ref,
    raw_caps, raw_tests, caps, tests, clips, acc, share, others,
    send_sem, recv_sem, tsend_sem, trecv_sem, bsend_sem, brecv_sem, local_sem,
):
    bank = lax.axis_index("bank")
    gal = lax.axis_index("gal")
    y_hi, core = bank // 2, bank % 2
    z, y_lo, x = gal // 8, (gal // 4) % 2, gal % 4
    y = y_hi * 2 + y_lo

    def at(axis, step):
        if axis == "x":
            return {"bank": bank, "gal": z * 8 + y_lo * 4 + (x + step + 4) % 4}
        if axis == "z":
            return {"bank": bank, "gal": ((z + step + 4) % 4) * 8 + y_lo * 4 + x}
        new_y = (y + step + 4) % 4
        return {"bank": (new_y // 2) * 2 + core, "gal": z * 8 + (new_y % 2) * 4 + x}

    partner = {"bank": bank, "gal": z * 8 + (1 - y_lo) * 4 + x}
    sibling = {"bank": y_hi * 2 + 1 - core, "gal": gal}

    barrier = pltpu.get_barrier_semaphore()
    peers = [at("x", 1), at("x", -1), at("z", 1), at("z", -1), at("y", 1), at("y", -1)]
    peers += [{"bank": (bank + k) % 4, "gal": gal} for k in (1, 2, 3)]
    for peer in peers:
        pl.semaphore_signal(barrier, inc=1, device_id=peer, device_id_type=MESH)

    load_caps = pltpu.make_async_copy(caps_ref, raw_caps, local_sem.at[3])
    load_tests = pltpu.make_async_copy(tests_ref, raw_tests, local_sem.at[4])
    load = pltpu.make_async_copy(gallery_ref, clips, local_sem.at[0])
    load_caps.start()
    load_tests.start()
    load.start()
    load_caps.wait()
    wide = raw_caps[...].astype(jnp.float32)
    unit = (wide * (unit_scale(wide) * exp2_scale)).astype(jnp.bfloat16)
    caps[0] = unit[0:PIECE, :]
    caps[1] = unit[PIECE : 2 * PIECE, :]
    load_tests.wait()
    wide = raw_tests[...].astype(jnp.float32)
    tests[bank, z, y_lo, x] = (wide * unit_scale(wide)).astype(jnp.bfloat16)
    acc[...] = jnp.zeros_like(acc)
    pl.semaphore_wait(barrier, len(peers))

    def send_of(source, target, axis, step):
        device = partner if axis == "y" else at(axis, step)
        return pltpu.make_async_remote_copy(
            src_ref=source,
            dst_ref=caps.at[target],
            send_sem=send_sem.at[target],
            recv_sem=recv_sem.at[target],
            device_id=device,
            device_id_type=MESH,
        )

    def forward(piece):
        for target, axis, step in CHILDREN[piece]:
            send_of(caps.at[piece], target, axis, step).start()

    def arrive(piece):
        send_of(caps.at[piece], piece, "x", 1).wait_recv()
        forward(piece)

    def block(step_y, step_z, first, last):
        yy, zz = (y + step_y + 4) % 4, (z + step_z + 4) % 4
        part = tests.at[(yy // 2) * 2 + core, zz, yy % 2]
        return part if last - first == 4 else part.at[pl.ds(first, last - first)]

    def test_message(index):
        if index < 3:
            step = (1, -1, 1)[index]
            offset = (0, 0, -1)[index]
            row = tests.at[bank, z, y_lo]
            return row.at[(x + offset + 4) % 4], row.at[(x + offset - step + 4) % 4], at("x", step)
        if index < 7:
            step = (1, -1, 1, -1)[index - 3]
            offset = (0, 0, -1, 1)[index - 3]
            first, last = ((0, 4), (0, 4), (0, 2), (2, 4))[index - 3]
            return block(0, offset, first, last), block(0, offset - step, first, last), at("z", step)
        if index < 23:
            zz = (0, -1, 1, 2)[(index - 7) // 4]
            kind = (index - 7) % 4
            step = (1, -1, 1, -1)[kind]
            offset = (0, 0, -1, 1)[kind]
            first, last = ((0, 4), (0, 4), (0, 2), (2, 4))[kind]
            return block(offset, zz, first, last), block(offset - step, zz, first, last), at("y", step)
        yy = (y + (0, 1, -1, 2)[index - 23] + 4) % 4
        low = (yy // 2) * 2
        return tests.at[low + core, :, yy % 2], tests.at[low + 1 - core, :, yy % 2], sibling

    def test_copy(index, arriving):
        sent, arrives, device = test_message(index)
        part = arrives if arriving else sent
        return pltpu.make_async_remote_copy(
            src_ref=part, dst_ref=part,
            send_sem=tsend_sem.at[index], recv_sem=trecv_sem.at[index],
            device_id=device, device_id_type=MESH,
        )

    def test_start(*indices):
        for index in indices:
            test_copy(index, False).start()

    def test_arrive(*indices):
        for index in indices:
            test_copy(index, True).wait_recv()

    test_start(0, 1)
    forward(0)
    forward(1)

    load.wait()

    def unit_block(index, carry):
        rows = pl.ds(pl.multiple_of(index * 256, 256), 256)
        wide = clips[rows, :].astype(jnp.float32)
        clips[rows, :] = (wide * unit_scale(wide)).astype(jnp.bfloat16)
        return carry

    lax.fori_loop(0, clips.shape[0] // 256, unit_block, 0)

    share_rows = columns_ref.shape[0]
    columns_copy = pltpu.make_async_copy(
        clips.at[pl.ds(pl.multiple_of(bank * share_rows, share_rows), share_rows), :],
        columns_ref,
        local_sem.at[1],
    )

    def move_tests(step):
        if step == 0:
            test_arrive(0, 1)
            test_start(2)
        if step == 2:
            test_arrive(2)
            test_start(3, 4, 7, 8)
        if step == 6:
            test_arrive(3, 4)
            test_start(5, 6, 11, 12, 15, 16)
            test_arrive(7, 8)
            test_start(9, 10)
        if step == 10:
            test_arrive(5, 6)
            test_start(19, 20)
            test_arrive(11, 12, 15, 16)
            test_start(13, 14, 17, 18)
        if step == 13:
            test_arrive(19, 20)
            test_start(21, 22, 23, 24, 25)

    def move(step):
        move_tests(step)
        for piece in HANDLED[step]:
            arrive(piece)
        if step == 1:
            columns_copy.start()

    def choose(step, low, high):
        if high - low == 1:
            move(low)
            return
        middle = (low + high) // 2

        @pl.when(step < middle)
        def _():
            choose(step, low, middle)

        @pl.when(step >= middle)
        def _():
            choose(step, middle, high)

    def one_step(step, carry):
        choose(step, 0, STEPS)
        block = caps[pl.ds(step * GROUP, GROUP)].reshape(GROUP * PIECE, D)
        sims = lax.dot_general(
            block, clips[...], (((1,), (1,)), ((), ())), preferred_element_type=jnp.float32
        )
        terms = jnp.exp2(sims).reshape(GROUP * PIECE // 8, 8, sims.shape[1])
        acc[...] += jnp.sum(terms, axis=0)
        return carry

    lax.fori_loop(0, STEPS, one_step, 0)

    sums = jnp.sum(acc[...], axis=0, keepdims=True)
    for k in range(4):
        share[k] = sums[:, k * share_rows : (k + 1) * share_rows]

    def bank_copy(k):
        peer = (bank + k) % 4
        return pltpu.make_async_remote_copy(
            src_ref=share.at[peer], dst_ref=others.at[k - 1],
            send_sem=bsend_sem.at[k - 1], recv_sem=brecv_sem.at[k - 1],
            device_id={"bank": peer, "gal": gal}, device_id_type=MESH,
        )

    for k in (2, 1, 3):
        bank_copy(k).start()

    test_arrive(9, 10, 13, 14, 17, 18, 21, 22)
    test_start(26)
    test_arrive(23, 24, 25, 26)
    tests_copy = pltpu.make_async_copy(tests, all_tests_ref, local_sem.at[2])
    tests_copy.start()

    for k in (1, 3, 2):
        bank_copy(k).wait_recv()
    total = share[bank] + others[0] + others[1] + others[2]
    count = 4 * 32 * caps_ref.shape[0]
    log_ref[...] = jnp.log(total / count)

    for k in (1, 2, 3):
        bank_copy(k).wait_send()
    for piece in range(PIECES):
        for target, axis, step in CHILDREN[piece]:
            send_of(caps.at[piece], target, axis, step).wait_send()
    for index in range(27):
        test_copy(index, False).wait_send()
    columns_copy.wait()
    tests_copy.wait()


def score_kernel(tests_ref, columns_ref, log_ref, out_ref):
    sims = lax.dot_general(
        tests_ref[...], columns_ref[...], (((1,), (1,)), ((), ())), preferred_element_type=jnp.float32
    )
    result = inverse_temp * sims - log_ref[...]
    out_ref[...] = result.reshape(out_ref.shape)


def local(querybank, gallery, test_queries):
    vmem = pl.BlockSpec(memory_space=pltpu.VMEM)
    anywhere = pl.BlockSpec(memory_space=pl.ANY)
    hbm = pl.BlockSpec(memory_space=pltpu.MemorySpace.HBM)
    bf16, f32 = jnp.bfloat16, jnp.float32
    clip_rows = gallery.shape[0]
    share_rows = clip_rows // 4
    test_rows = test_queries.shape[0] * 128
    tests_shape = (4, 4, 2, 4, test_queries.shape[0], D)
    every_test, columns, logs = pl.pallas_call(
        gather_kernel,
        out_shape=(
            jax.ShapeDtypeStruct(tests_shape, bf16),
            jax.ShapeDtypeStruct((share_rows, D), bf16),
            jax.ShapeDtypeStruct((1, share_rows), f32),
        ),
        in_specs=[hbm, hbm, hbm],
        out_specs=(anywhere, anywhere, vmem),
        scratch_shapes=[
            pltpu.VMEM(querybank.shape, bf16),
            pltpu.VMEM(test_queries.shape, bf16),
            pltpu.VMEM((PIECES, PIECE, D), bf16),
            pltpu.VMEM(tests_shape, bf16),
            pltpu.VMEM((clip_rows, D), bf16),
            pltpu.VMEM((8, clip_rows), f32),
            pltpu.VMEM((4, 1, share_rows), f32),
            pltpu.VMEM((3, 1, share_rows), f32),
            pltpu.SemaphoreType.DMA((PIECES,)),
            pltpu.SemaphoreType.DMA((PIECES,)),
            pltpu.SemaphoreType.DMA((27,)),
            pltpu.SemaphoreType.DMA((27,)),
            pltpu.SemaphoreType.DMA((3,)),
            pltpu.SemaphoreType.DMA((3,)),
            pltpu.SemaphoreType.DMA((5,)),
        ],
        compiler_params=pltpu.CompilerParams(
            collective_id=0, has_side_effects=True, vmem_limit_bytes=40 << 20
        ),
    )(*(pltpu.with_memory_space_constraint(a, pltpu.MemorySpace.HBM) for a in (querybank, test_queries, gallery)))
    block = 256
    result = pl.pallas_call(
        score_kernel,
        grid=(test_rows // block,),
        out_shape=jax.ShapeDtypeStruct((test_rows, 1, share_rows), f32),
        in_specs=[
            pl.BlockSpec((block, D), lambda i: (i, 0)),
            pl.BlockSpec((share_rows, D), lambda i: (0, 0)),
            pl.BlockSpec((1, share_rows), lambda i: (0, 0)),
        ],
        out_specs=pl.BlockSpec((block, 1, share_rows), lambda i: (i, 0, 0)),
        compiler_params=pltpu.CompilerParams(vmem_limit_bytes=40 << 20),
    )(every_test.reshape(test_rows, D), columns, logs)
    return result


def solution(mesh):
    placed = (P(("bank", "gal"), None), P("gal", None), P(("bank", "gal"), None))
    return jax.shard_map(
        local, mesh=mesh, in_specs=placed, out_specs=P(None, "gal", "bank"), check_vma=False
    )
```

```python
import functools
import math

import jax
import jax.numpy as jnp
from jax import lax
from jax.experimental import pallas as pl
from jax.experimental.pallas import tpu as pltpu
from jax.sharding import PartitionSpec as P

MESH = pl.DeviceIdType.MESH
inverse_temp = 20.0
epsilon = 1e-06
exp2_scale = inverse_temp * math.log2(math.e)

D = 512
PIECE = 64
SIZES = (2,) + 7 * (4,) + 4 * (8,) + (2,)
RING = 4


ORDER = (
    0, 1, 32, 33, 25, 6, 24, 2, 34, 8, 9, 4, 3, 57, 31, 56,
    39, 40, 27, 35, 14, 41, 15, 10, 63, 17, 26, 11, 49, 7, 46, 48,
    59, 42, 38, 16, 30, 43, 58, 12, 47, 5, 51, 19, 18, 13, 22, 50,
    23, 55, 54, 45, 62, 61, 60, 20, 44, 28, 29, 37, 36, 21, 52, 53,
)
AHEAD = (
    0, 0, 1, 0, 0, 0, 0, 2, 0, 1, 2, 0, 2, 0, 0, 0,
    0, 1, 0, 0, 0, 1, 0, 0, 0, 0, 0, 0, 0, 0, 0, 0,
    1, 0, 0, 1, 0, 0, 0, 0, 0, 0, 0, 0, 0, 0, 0, 0,
    0, 0, 0, 0, 1, 0, 0, 0, 1, 0, 1, 0, 0, 0, 0, 0,
)


def piece_table():
    pieces = [(code % 2, code // 32, code // 8 % 4, code // 2 % 4) for code in ORDER]

    def way(piece):
        kind, dy, p1, p2 = piece
        if p2:
            side = p2 if p2 != 2 else (1 if (dy + p1) % 2 == 0 else 3)
            parent = (kind, dy, p1, (p2 - side) % RING)
            return parent, ("x", "z")[1 - kind], side
        if p1:
            side = p1 if p1 != 2 else (1 if dy == 0 else 3)
            parent = (kind, dy, (p1 - side) % RING, 0)
            return parent, ("x", "z")[kind], side
        if dy:
            return (kind, 0, 0, 0), "y", 1
        return None

    slot = {q: s for s, q in enumerate(pieces)}
    children = [[] for _ in pieces]
    for q in pieces:
        came = way(q)
        if came is not None:
            parent, axis, side = came
            children[slot[parent]].append((slot[q], axis, -side))
    return children


CHILDREN = piece_table()
PIECES = len(CHILDREN)
STEPS = len(SIZES)
FIRSTS = [sum(SIZES[:step]) for step in range(STEPS)]
STEP_OF = [step for step in range(STEPS) for unused in range(SIZES[step])]
HANDLED = [
    [s for s in range(2, PIECES) if max(0, STEP_OF[s] - AHEAD[s]) == step] for step in range(STEPS)
]


def unit_scale(wide):
    return lax.rsqrt(jnp.sum(wide * wide, axis=-1, keepdims=True) + epsilon)


def gather_kernel(
    caps_ref, tests_ref, gallery_ref, scores_ref, log_ref,
    raw_caps, raw_tests, caps, tests, clips, acc, share, others,
    send_sem, recv_sem, tsend_sem, trecv_sem, bsend_sem, brecv_sem, local_sem,
):
    bank = lax.axis_index("bank")
    gal = lax.axis_index("gal")
    y_hi, core = bank // 2, bank % 2
    z, y_lo, x = gal // 8, (gal // 4) % 2, gal % 4
    y = y_hi * 2 + y_lo

    def at(axis, step):
        if axis == "x":
            return {"bank": bank, "gal": z * 8 + y_lo * 4 + (x + step + 4) % 4}
        if axis == "z":
            return {"bank": bank, "gal": ((z + step + 4) % 4) * 8 + y_lo * 4 + x}
        new_y = (y + step + 4) % 4
        return {"bank": (new_y // 2) * 2 + core, "gal": z * 8 + (new_y % 2) * 4 + x}

    partner = {"bank": bank, "gal": z * 8 + (1 - y_lo) * 4 + x}
    sibling = {"bank": y_hi * 2 + 1 - core, "gal": gal}

    barrier = pltpu.get_barrier_semaphore()
    peers = [at("x", 1), at("x", -1), at("z", 1), at("z", -1), at("y", 1), at("y", -1)]
    peers += [{"bank": (bank + k) % 4, "gal": gal} for k in (1, 2, 3)]
    for peer in peers:
        pl.semaphore_signal(barrier, inc=1, device_id=peer, device_id_type=MESH)

    load_caps = pltpu.make_async_copy(caps_ref, raw_caps, local_sem.at[3])
    load_tests = pltpu.make_async_copy(tests_ref, raw_tests, local_sem.at[4])
    load = pltpu.make_async_copy(gallery_ref, clips, local_sem.at[0])
    load_caps.start()
    load_tests.start()
    load.start()
    load_caps.wait()
    wide = raw_caps[...].astype(jnp.float32)
    unit = (wide * (unit_scale(wide) * exp2_scale)).astype(jnp.bfloat16)
    caps[0] = unit[0:PIECE, :]
    caps[1] = unit[PIECE : 2 * PIECE, :]
    load_tests.wait()
    wide = raw_tests[...].astype(jnp.float32)
    tests[bank, z, y_lo, x] = (wide * unit_scale(wide)).astype(jnp.bfloat16)
    acc[...] = jnp.zeros_like(acc)
    pl.semaphore_wait(barrier, len(peers))

    def send_of(source, target, axis, step):
        device = partner if axis == "y" else at(axis, step)
        return pltpu.make_async_remote_copy(
            src_ref=source,
            dst_ref=caps.at[target],
            send_sem=send_sem.at[target],
            recv_sem=recv_sem.at[target],
            device_id=device,
            device_id_type=MESH,
        )

    def forward(piece):
        for target, axis, step in CHILDREN[piece]:
            send_of(caps.at[piece], target, axis, step).start()

    def arrive(piece):
        send_of(caps.at[piece], piece, "x", 1).wait_recv()
        forward(piece)

    def block(step_y, step_z, first, last):
        yy, zz = (y + step_y + 4) % 4, (z + step_z + 4) % 4
        part = tests.at[(yy // 2) * 2 + core, zz, yy % 2]
        return part if last - first == 4 else part.at[pl.ds(first, last - first)]

    def test_message(index):
        if index < 3:
            step = (1, -1, 1)[index]
            offset = (0, 0, -1)[index]
            row = tests.at[bank, z, y_lo]
            return row.at[(x + offset + 4) % 4], row.at[(x + offset - step + 4) % 4], at("x", step)
        if index < 7:
            step = (1, -1, 1, -1)[index - 3]
            offset = (0, 0, -1, 1)[index - 3]
            first, last = ((0, 4), (0, 4), (0, 2), (2, 4))[index - 3]
            return block(0, offset, first, last), block(0, offset - step, first, last), at("z", step)
        if index < 23:
            zz = (0, -1, 1, 2)[(index - 7) // 4]
            kind = (index - 7) % 4
            step = (1, -1, 1, -1)[kind]
            offset = (0, 0, -1, 1)[kind]
            first, last = ((0, 4), (0, 4), (0, 2), (2, 4))[kind]
            return block(offset, zz, first, last), block(offset - step, zz, first, last), at("y", step)
        yy = (y + (0, 1, -1, 2)[index - 23] + 4) % 4
        low = (yy // 2) * 2
        return tests.at[low + core, :, yy % 2], tests.at[low + 1 - core, :, yy % 2], sibling

    def test_copy(index, arriving):
        sent, arrives, device = test_message(index)
        part = arrives if arriving else sent
        return pltpu.make_async_remote_copy(
            src_ref=part, dst_ref=part,
            send_sem=tsend_sem.at[index], recv_sem=trecv_sem.at[index],
            device_id=device, device_id_type=MESH,
        )

    def test_start(*indices):
        for index in indices:
            test_copy(index, False).start()

    def test_arrive(*indices):
        for index in indices:
            test_copy(index, True).wait_recv()

    test_start(0, 1)
    forward(0)
    forward(1)

    load.wait()

    def unit_block(index, carry):
        rows = pl.ds(pl.multiple_of(index * 256, 256), 256)
        wide = clips[rows, :].astype(jnp.float32)
        clips[rows, :] = (wide * unit_scale(wide)).astype(jnp.bfloat16)
        return carry

    lax.fori_loop(0, clips.shape[0] // 256, unit_block, 0)

    share_rows = log_ref.shape[1]

    def move_tests(step):
        if step == 0:
            test_arrive(0, 1)
            test_start(2)
        if step == 2:
            test_arrive(2)
            test_start(3, 4, 7, 8)
        if step == 7:
            test_arrive(3, 4)
            test_start(5, 6, 11, 12, 15, 16)
            test_arrive(7, 8)
            test_start(9, 10)
        if step == 9:
            test_arrive(5, 6)
            test_start(19, 20)
            test_arrive(11, 12, 15, 16)
            test_start(13, 14, 17, 18)
        if step == 11:
            test_arrive(19, 20)
            test_start(21, 22, 23, 24, 25)

    def move(step):
        move_tests(step)
        for piece in HANDLED[step]:
            arrive(piece)

    def choose(step, low, high):
        if high - low == 1:
            move(low)
            return
        middle = (low + high) // 2

        @pl.when(step < middle)
        def _():
            choose(step, low, middle)

        @pl.when(step >= middle)
        def _():
            choose(step, middle, high)

    def multiply(first, count):
        rows = caps[pl.ds(first, count)].reshape(count * PIECE, D)
        sims = lax.dot_general(
            rows, clips[...], (((1,), (1,)), ((), ())), preferred_element_type=jnp.float32
        )
        terms = jnp.exp2(sims).reshape(count * PIECE // 8, 8, sims.shape[1])
        acc[...] += jnp.sum(terms, axis=0)

    def run_steps(low, high):
        if high - low == 1:
            move(low)
            multiply(FIRSTS[low], SIZES[low])
            return

        def one_step(step, carry):
            choose(step, low, high)
            multiply(FIRSTS[low] + (step - low) * SIZES[low], SIZES[low])
            return carry

        lax.fori_loop(low, high, one_step, 0)

    run_steps(0, 1)
    run_steps(1, 8)
    run_steps(8, 12)
    run_steps(12, 13)

    sums = jnp.sum(acc[...], axis=0, keepdims=True)
    for k in range(4):
        share[k] = sums[:, k * share_rows : (k + 1) * share_rows]

    def bank_copy(k):
        peer = (bank + k) % 4
        return pltpu.make_async_remote_copy(
            src_ref=share.at[peer], dst_ref=others.at[k - 1],
            send_sem=bsend_sem.at[k - 1], recv_sem=brecv_sem.at[k - 1],
            device_id={"bank": peer, "gal": gal}, device_id_type=MESH,
        )

    for k in (2, 1, 3):
        bank_copy(k).start()

    test_arrive(9, 10, 13, 14, 17, 18, 21, 22)
    test_start(26)
    mine = pl.ds(pl.multiple_of(bank * share_rows, share_rows), share_rows)

    def score_block(step, carry):
        index = 2 * (step % 2) + (core + step // 2) % 2

        @pl.when(step == 2)
        def _():
            test_arrive(23, 24, 25, 26)

        rows = tests[index].reshape(scores_ref.shape[0] // 4, D)
        sims = lax.dot_general(
            rows, clips[mine, :], (((1,), (1,)), ((), ())), preferred_element_type=jnp.float32
        )
        block_rows = pl.ds(index * rows.shape[0], rows.shape[0])
        scores_ref[block_rows] = (inverse_temp * sims).reshape(rows.shape[0], 1, share_rows)
        return carry

    lax.fori_loop(0, 4, score_block, 0)

    for k in (1, 3, 2):
        bank_copy(k).wait_recv()
    total = share[bank] + others[0] + others[1] + others[2]
    count = 4 * 32 * caps_ref.shape[0]
    log_ref[...] = jnp.log(total / count)

    for k in (1, 2, 3):
        bank_copy(k).wait_send()
    for piece in range(PIECES):
        for target, axis, step in CHILDREN[piece]:
            send_of(caps.at[piece], target, axis, step).wait_send()
    for index in range(27):
        test_copy(index, False).wait_send()


def score_kernel(scores_ref, log_ref, out_ref):
    rows = out_ref.shape[0]
    block = scores_ref[pl.ds(pl.multiple_of(pl.program_id(0) * rows, rows), rows)]
    out_ref[...] = block - log_ref[...].reshape(1, 1, log_ref.shape[1])


def local(querybank, gallery, test_queries):
    vmem = pl.BlockSpec(memory_space=pltpu.VMEM)
    hbm = pl.BlockSpec(memory_space=pltpu.MemorySpace.HBM)
    bf16, f32 = jnp.bfloat16, jnp.float32
    clip_rows = gallery.shape[0]
    share_rows = clip_rows // 4
    test_rows = test_queries.shape[0] * 128
    tests_shape = (4, 4, 2, 4, test_queries.shape[0], D)
    scores, logs = pl.pallas_call(
        gather_kernel,
        out_shape=(
            jax.ShapeDtypeStruct((test_rows, 1, share_rows), f32),
            jax.ShapeDtypeStruct((1, share_rows), f32),
        ),
        in_specs=[hbm, hbm, hbm],
        out_specs=(vmem, vmem),
        scratch_shapes=[
            pltpu.VMEM(querybank.shape, bf16),
            pltpu.VMEM(test_queries.shape, bf16),
            pltpu.VMEM((PIECES, PIECE, D), bf16),
            pltpu.VMEM(tests_shape, bf16),
            pltpu.VMEM((clip_rows, D), bf16),
            pltpu.VMEM((8, clip_rows), f32),
            pltpu.VMEM((4, 1, share_rows), f32),
            pltpu.VMEM((3, 1, share_rows), f32),
            pltpu.SemaphoreType.DMA((PIECES,)),
            pltpu.SemaphoreType.DMA((PIECES,)),
            pltpu.SemaphoreType.DMA((27,)),
            pltpu.SemaphoreType.DMA((27,)),
            pltpu.SemaphoreType.DMA((3,)),
            pltpu.SemaphoreType.DMA((3,)),
            pltpu.SemaphoreType.DMA((5,)),
        ],
        compiler_params=pltpu.CompilerParams(
            collective_id=0, has_side_effects=True, vmem_limit_bytes=40 << 20
        ),
    )(*(pltpu.with_memory_space_constraint(a, pltpu.MemorySpace.HBM) for a in (querybank, test_queries, gallery)))
    block = 512
    result = pl.pallas_call(
        score_kernel,
        grid=(test_rows // block,),
        out_shape=jax.ShapeDtypeStruct((test_rows, 1, share_rows), f32),
        in_specs=[
            vmem,
            vmem,
        ],
        out_specs=pl.BlockSpec((block, 1, share_rows), lambda i: (i, 0, 0)),
        compiler_params=pltpu.CompilerParams(vmem_limit_bytes=40 << 20),
    )(scores, logs)
    return result


def solution(mesh):
    placed = (P(("bank", "gal"), None), P("gal", None), P(("bank", "gal"), None))
    return jax.shard_map(
        local, mesh=mesh, in_specs=placed, out_specs=P(None, "gal", "bank"), check_vma=False
    )
```
